32 devices in a mesh: member: 2 (over x), gx: 16 (over z, y, core).
Axes of the slice: x: 2, y: 2, z: 4, core: 2. Of those that a mesh axis runs over, the one named last changes fastest.
Arguments:
- electric: float32 [3, 64, 256, 128], P(None, 'gx'), may hold values from -6 to 6
- magnetic: float32 [3, 64, 256, 128], P(None, 'gx'), may hold values from -6 to 6
- material: int32 [128, 256, 128], P(('member', 'gx')), parts along dimension 0, may hold values from 0 to 3, as said below
- permittivity: float32 [4], replicated, may hold values from 1 to 4
- pole_frequency: float32 [2], replicated, may hold values from 0.3 to 1.2
- pole_damping: float32 [2], replicated, may hold values from 0.05 to 1
- pole_strength: float32 [2], replicated, may hold values from 0.3 to 2
- frequencies: float32 [8], replicated, may hold values from 0.2 to 2
- plane_depth: int32 [4], replicated, may hold values from 1 to 126
- mode_fields: float32 [4, 4, 64, 256], P(None, None, 'gx'), may hold values from -40 to 40
Outputs:
- electric_final: float32 [3, 128, 256, 128], P(None, ('member', 'gx')), parts along dimension 1
- magnetic_final: float32 [3, 128, 256, 128], P(None, ('member', 'gx')), parts along dimension 1
- monitors: float32 [2, 4, 8, 4, 128, 256], P(None, None, None, None, ('member', 'gx')), parts along dimension 4
- intersection: float32 [4, 4, 8], P('member'), parts along dimension 0
The draws below stay inside these ranges and needn't reach their ends.
There are 2 independent parts, one for each index of `member`. The reference program is written for one: setup_inputs(seed, part) draws one part's arguments, and reference() takes and returns one part's arrays. A program takes and returns all parts, laid end to end along the dimension named above; an argument that names none is the same for every part. Nothing has to cross between parts.
Inputs may be any that keep to these rules, and one draw needn't show every extreme that they name: Each 16-layer thickness profile stacks layers along the first dimension, each of one material, with a lateral lattice of material 0 cells in some layers; materials 2 and above are dispersive.
All inputs are finite; a program needn't handle non-finite values.
Results may differ from the reference program's by a relative error of at most 0.0003.
Values sent between devices are 32-bit elements; how exact they have to be, the bound alone decides.
A program may use at most 64 MiB of HBM per device.

```python
import math
import jax
import jax.numpy as jnp
from jax import lax

NY = 256
NZ = 128
STEPS = 6
NF = 8
NMON = 4
LAYERS = 16
NMAT = 4
NPOLE = 2
NX = 64


def draw_material(key, part):
    keys = jax.random.split(jax.random.fold_in(key, 11), 4)
    cuts = jax.random.permutation(keys[0], NX - 1)[:LAYERS - 1] + 1
    position = jnp.arange(NX, dtype=jnp.int32)
    layer = jnp.sum((position[:, None] >= cuts[None, :]).astype(jnp.int32), axis=1)
    layer_kind = (jax.random.permutation(keys[1], LAYERS) % NMAT).astype(jnp.int32)
    patterned = jax.random.randint(keys[2], (LAYERS,), 0, 2)
    holes = jax.random.randint(keys[3], (NY, NZ), 0, 2)
    kind_cells = jnp.take(layer_kind, layer)
    drilled = jnp.take(patterned, layer)
    filled = kind_cells[:, None, None] * jnp.ones((1, NY, NZ), jnp.int32)
    return jnp.where(drilled[:, None, None] * holes[None, :, :] > 0, 0, filled).astype(jnp.int32)


def draw_mode_fields(key, part):
    ramp = 1.0 + 2.0 * jnp.arange(NX, dtype=jnp.float32) / (NX - 1.0)
    base = jnp.clip(jax.random.normal(jax.random.fold_in(key, 7), (4, NMON, NX, NY), jnp.float32), -4.0, 4.0)
    return base * ramp[None, None, :, None]


def set_ends(result, own_key, low, largest):
    longest = result.shape.index(max(result.shape))
    spots = []
    for shift in (0, 1):
        where = [jax.random.randint(jax.random.fold_in(own_key, axis), (), 0, length) for axis, length in enumerate(result.shape)]
        where[longest] = (where[longest] + shift) % result.shape[longest]
        spots.append(tuple(where))
    return result.at[spots[0]].set(low).at[spots[1]].set(largest)


def shard_levels(own_key, shape, cuts, low, top_value):
    gain, own = 1.0, jax.random.fold_in(own_key, 6)
    for dim, parts in cuts:
        steps = jnp.exp(jax.random.uniform(jax.random.fold_in(own, dim), (parts,), jnp.float32, low / len(cuts), top_value / len(cuts)))
        gain = gain * jnp.repeat(steps, shape[dim] // parts).reshape([-1 if axis == dim else 1 for axis in range(len(shape))])
    return gain


def noise(rng, extent, scale, reach, shards=(), kind=jnp.bfloat16):
    entries = scale * jax.random.normal(rng, extent, jnp.float32)
    if shards:
        entries = entries * shard_levels(rng, extent, shards, -0.22, 0.18)
    return jnp.clip(entries, -reach, reach).astype(kind)


def setup_inputs(seed: int = 0, part: int = 0) -> dict:
    arg_keys = jax.random.split(jax.random.key(seed), 11)
    part_keys = jax.random.split(jax.random.fold_in(arg_keys[10], part), 11)
    return {
        "electric": noise(arg_keys[0], (3, NX, NY, NZ), 1.0, 6.0, ((1, 16),), jnp.float32),
        "magnetic": noise(arg_keys[1], (3, NX, NY, NZ), 1.0, 6.0, ((1, 16),), jnp.float32),
        "material": draw_material(jax.random.fold_in(jax.random.fold_in(arg_keys[10], part), 71), part),
        "permittivity": jnp.clip(jax.random.uniform(arg_keys[3], (NMAT,), jnp.float32, 1.0, 4.0), 1.0, 4.0),
        "pole_frequency": jnp.clip(jnp.exp(jax.random.uniform(arg_keys[4], (NPOLE,), jnp.float32, math.log(0.3), math.log(1.2))), 0.3, 1.2),
        "pole_damping": jnp.clip(jnp.exp(jax.random.uniform(arg_keys[5], (NPOLE,), jnp.float32, math.log(0.05), math.log(1.0))), 0.05, 1.0),
        "pole_strength": jnp.clip(jnp.exp(jax.random.uniform(arg_keys[6], (NPOLE,), jnp.float32, math.log(0.3), math.log(2.0))), 0.3, 2.0),
        "frequencies": jnp.clip(jnp.exp(jax.random.uniform(arg_keys[7], (NF,), jnp.float32, math.log(0.2), math.log(2.0))), 0.2, 2.0),
        "plane_depth": set_ends(jax.random.randint(arg_keys[8], (NMON,), 1, NZ - 1), jax.random.fold_in(arg_keys[8], 1), 1, (NZ - 1) - 1).astype(jnp.int32),
        "mode_fields": draw_mode_fields(jax.random.fold_in(arg_keys[10], 71), part),
    }


DT = 0.5

def zero_rim(field, direction):
    return jnp.zeros_like(lax.slice_in_dim(field, 0, 1, axis=direction))

def diff_ahead(field, direction, beyond):
    remainder = lax.slice_in_dim(field, 1, field.shape[direction], axis=direction)
    return jnp.concatenate([remainder, beyond], axis=direction) - field

def diff_behind(field, direction, preceding):
    remainder = lax.slice_in_dim(field, 0, field.shape[direction] - 1, axis=direction)
    return field - jnp.concatenate([preceding, remainder], axis=direction)

def ahead_open(field, direction):
    return diff_ahead(field, direction, zero_rim(field, direction))

def behind_open(field, direction):
    return diff_behind(field, direction, zero_rim(field, direction))

def curl_e(e_field, upper):
    first = ahead_open(e_field[2], 1) - ahead_open(e_field[1], 2)
    second = ahead_open(e_field[0], 2) - diff_ahead(e_field[2], 0, upper[1])
    third = diff_ahead(e_field[1], 0, upper[0]) - ahead_open(e_field[0], 1)
    return jnp.stack([first, second, third])

def curl_h(h_field, lower):
    first = behind_open(h_field[2], 1) - behind_open(h_field[1], 2)
    second = behind_open(h_field[0], 2) - diff_behind(h_field[2], 0, lower[1])
    third = diff_behind(h_field[1], 0, lower[0]) - behind_open(h_field[0], 1)
    return jnp.stack([first, second, third])

def coefficients(material, permittivity, pole_frequency, pole_damping, pole_strength):
    eps_cell = jnp.zeros(material.shape, jnp.float32)
    for kind_index in range(permittivity.shape[0]):
        eps_cell = eps_cell + jnp.where(material == kind_index, permittivity[kind_index], 0.0)
    damping = jnp.zeros(material.shape, jnp.float32)
    square = jnp.zeros(material.shape, jnp.float32)
    driving = jnp.zeros(material.shape, jnp.float32)
    offset = permittivity.shape[0] - pole_frequency.shape[0]
    for pole_index in range(pole_frequency.shape[0]):
        chosen = material == pole_index + offset
        freq_sq = pole_frequency[pole_index] * pole_frequency[pole_index]
        damping = damping + jnp.where(chosen, pole_damping[pole_index], 0.0)
        square = square + jnp.where(chosen, freq_sq, 0.0)
        driving = driving + jnp.where(chosen, pole_strength[pole_index] * freq_sq, 0.0)
    divisor = 1.0 + 0.5 * DT * damping
    retain = (1.0 - 0.5 * DT * damping) / divisor
    pulling = DT * driving / divisor
    spring = DT * square / divisor
    step_e = DT / eps_cell
    return (retain, pulling, spring, step_e)

def record(monitors, e_field, h_field, select, frequencies, step):
    plane_e = jnp.einsum('cxyz,zm->cmxy', e_field[:2], select, precision=lax.Precision.HIGHEST)
    plane_h = jnp.einsum('cxyz,zm->cmxy', h_field[:2], select, precision=lax.Precision.HIGHEST)
    planes = jnp.concatenate([plane_e, plane_h], axis=0)
    phase_e = (step + 1.0) * DT * frequencies
    phase_h = (step + 0.5) * DT * frequencies
    cosines = jnp.stack([jnp.cos(phase_e), jnp.cos(phase_e), jnp.cos(phase_h), jnp.cos(phase_h)])
    sine_part = -jnp.stack([jnp.sin(phase_e), jnp.sin(phase_e), jnp.sin(phase_h), jnp.sin(phase_h)])
    rotation = jnp.stack([cosines, sine_part])
    return monitors + rotation[:, :, :, None, None, None] * planes[None, :, None, :, :, :]

def project(monitors, mode_fields, scale):
    pairing = jnp.stack([mode_fields[3], -mode_fields[2], -mode_fields[1], mode_fields[0]])
    return scale * jnp.einsum('rcfmxy,cmxy->rmf', monitors, pairing, precision=lax.Precision.HIGHEST)

def reference(electric, magnetic, material, permittivity, pole_frequency, pole_damping, pole_strength, frequencies, plane_depth, mode_fields):
    retain, pulling, spring, step_e = coefficients(material, permittivity, pole_frequency, pole_damping, pole_strength)
    select = (jnp.arange(NZ)[:, None] == plane_depth[None, :]).astype(jnp.float32)
    boundary = jnp.zeros((2, 1, NY, NZ), jnp.float32)
    current = jnp.zeros_like(electric)
    polarized = jnp.zeros_like(electric)
    monitors = jnp.zeros((2, 4, NF, NMON, NX, NY), jnp.float32)
    for step in range(STEPS):
        magnetic = magnetic - DT * curl_e(electric, boundary)
        current = retain * current + pulling * electric - spring * polarized
        polarized = polarized + DT * current
        electric = electric + step_e * (curl_h(magnetic, boundary) - current)
        monitors = record(monitors, electric, magnetic, select, frequencies, step)
    intersection = project(monitors, mode_fields, 1.0 / math.sqrt(4.0 * NX * NY))
    return (electric, magnetic, monitors, intersection)
```

```python
import functools
import math

import jax
import jax.numpy as jnp
from jax import lax
from jax.experimental import pallas as pl
from jax.experimental.pallas import tpu as pltpu
from jax.sharding import PartitionSpec as P

STEPS = 6
DT = 0.5
CHUNKS = 4
ROWS = 32
PAD = 8
MESH = pl.DeviceIdType.MESH
F32 = jnp.float32
BF16 = jnp.bfloat16


def ahead(value):
    width = value.shape[-1]
    lane = lax.broadcasted_iota(jnp.int32, value.shape, 1)
    return jnp.where(lane == width - 1, 0.0, pltpu.roll(value, width - 1, 1))


def behind(value):
    lane = lax.broadcasted_iota(jnp.int32, value.shape, 1)
    return jnp.where(lane == 0, 0.0, pltpu.roll(value, 1, 1))


def main_kernel(
    count,
    scale,
    perm_ref,
    freq_ref,
    damp_ref,
    strength_ref,
    depth_ref,
    rot_ref,
    rotv_ref,
    mode_ref,
    el_ref,
    ma_ref,
    mat_ref,
    el_out,
    ma_out,
    mon_ref,
    inter_ref,
    eb,
    hb,
    ge,
    gh,
    jb,
    pb,
    coef,
    matb,
    planes,
    pick,
    part,
    gathered,
    in_sem,
    out_sem,
    se_sem,
    re_sem,
    sh_sem,
    rh_sem,
    sp_sem,
    rp_sem,
):
    me = lax.axis_index("gx")
    layers, width = mat_ref.shape[0], mat_ref.shape[1]
    chunk = width // CHUNKS
    has_upper = me < count - 1
    has_lower = me > 0
    top = layers - 1

    barrier = pltpu.get_barrier_semaphore()
    for k in range(1, count):
        pl.semaphore_signal(
            barrier, inc=1, device_id={"gx": lax.rem(me + k, count)}, device_id_type=MESH
        )

    loads = [
        pltpu.make_async_copy(mat_ref, matb, in_sem.at[0]),
        pltpu.make_async_copy(el_ref, eb.at[:, :, pl.ds(0, width)], in_sem.at[1]),
        pltpu.make_async_copy(ma_ref, hb.at[:, :, pl.ds(PAD, width)], in_sem.at[2]),
    ]
    for load in loads:
        load.start()

    def send_e(c, source):
        rows = pl.ds(c * chunk, chunk)
        return pltpu.make_async_remote_copy(
            src_ref=source.at[pl.ds(1, 2), 0, rows],
            dst_ref=ge.at[:, rows],
            send_sem=se_sem.at[c],
            recv_sem=re_sem.at[c],
            device_id={"gx": me - 1},
            device_id_type=MESH,
        )

    def send_h(c):
        return pltpu.make_async_remote_copy(
            src_ref=hb.at[pl.ds(1, 2), top, pl.ds(PAD + c * chunk, chunk)],
            dst_ref=gh.at[:, pl.ds(c * chunk, chunk)],
            send_sem=sh_sem.at[c],
            recv_sem=rh_sem.at[c],
            device_id={"gx": me + 1},
            device_id_type=MESH,
        )

    nm = depth_ref.shape[0]
    deep = mat_ref.shape[2]
    shape = pick.shape
    row = lax.broadcasted_iota(jnp.int32, shape, 0)
    col = lax.broadcasted_iota(jnp.int32, shape, 1)
    wanted = jnp.zeros(shape, jnp.int32)
    for m in range(nm):
        wanted = jnp.where(row // 8 == m, depth_ref[m], wanted)
    hit = (row % 8 == col // (2 * deep)) & (col % deep == wanted)
    pick[...] = jnp.where(hit, 1.0, 0.0).astype(BF16)

    zero_rows = jnp.zeros((PAD, deep), F32)
    for c in range(3):
        for x in range(layers):
            eb[c, x, pl.ds(width, PAD), :] = zero_rows
            hb[c, x, pl.ds(0, PAD), :] = zero_rows

    @pl.when(jnp.logical_not(has_upper))
    def _():
        ge[...] = jnp.zeros_like(ge)

    @pl.when(jnp.logical_not(has_lower))
    def _():
        gh[...] = jnp.zeros_like(gh)

    kinds = perm_ref.shape[0]
    offset = kinds - freq_ref.shape[0]
    ones = jnp.ones((8, deep), F32)
    tables = []
    for kind in range(kinds):
        if kind < offset:
            g, w2, drive = 0.0 * ones, 0.0 * ones, 0.0 * ones
        else:
            p = kind - offset
            g = damp_ref[p] * ones
            w2 = (freq_ref[p] * ones) * freq_ref[p]
            drive = strength_ref[p] * w2
        divisor = 1.0 + 0.5 * DT * g
        tables.append(
            (
                (1.0 - 0.5 * DT * g) / divisor,
                DT * drive / divisor,
                DT * w2 / divisor,
                DT / (perm_ref[kind] * ones),
            )
        )

    loads[0].wait()
    for x in range(layers):

        def fill(b, carry, x=x):
            rows = pl.ds(pl.multiple_of(b * 8, 8), 8)
            q = matb[x, rows, :]
            for i in range(4):
                value = tables[0][i]
                for kind in range(1, kinds):
                    value = jnp.where(q == kind, tables[kind][i], value)
                coef[i, x, rows, :] = value
            zero = jnp.zeros_like(ones)
            for c in range(3):
                jb[c, x, rows, :] = zero
                pb[c, x, rows, :] = zero
            return carry

        lax.fori_loop(0, width // 8, fill, 0, unroll=2)

    pl.semaphore_wait(barrier, count - 1)

    @pl.when(has_lower)
    def _():
        for c in range(CHUNKS):
            send_e(c, el_ref).start()

    loads[1].wait()
    loads[2].wait()

    def update_h(x, y):
        here, next_y = pl.ds(y, ROWS), pl.ds(y + 1, ROWS)
        spot = pl.ds(y + PAD, ROWS)
        ex, ey, ez = eb[0, x, here, :], eb[1, x, here, :], eb[2, x, here, :]
        ex_y, ez_y = eb[0, x, next_y, :], eb[2, x, next_y, :]
        if x < top:
            ey_x, ez_x = eb[1, x + 1, here, :], eb[2, x + 1, here, :]
        else:
            ey_x, ez_x = ge[0, here, :], ge[1, here, :]
        hb[0, x, spot, :] -= DT * ((ez_y - ez) - (ahead(ey) - ey))
        hb[1, x, spot, :] -= DT * ((ahead(ex) - ex) - (ez_x - ez))
        hb[2, x, spot, :] -= DT * ((ey_x - ey) - (ex_y - ex))

    def update_e(x, y):
        here = pl.ds(y, ROWS)
        spot, last_y = pl.ds(y + PAD, ROWS), pl.ds(y + PAD - 1, ROWS)
        hx, hy, hz = hb[0, x, spot, :], hb[1, x, spot, :], hb[2, x, spot, :]
        hx_y, hz_y = hb[0, x, last_y, :], hb[2, x, last_y, :]
        if x > 0:
            hy_x, hz_x = hb[1, x - 1, spot, :], hb[2, x - 1, spot, :]
        else:
            hy_x, hz_x = gh[0, here, :], gh[1, here, :]
        curl = (
            (hz - hz_y) - (hy - behind(hy)),
            (hx - behind(hx)) - (hz - hz_x),
            (hy - hy_x) - (hx - hx_y),
        )
        retain, pulling = coef[0, x, here, :], coef[1, x, here, :]
        spring, step_e = coef[2, x, here, :], coef[3, x, here, :]
        for c in range(3):
            field, polar = eb[c, x, here, :], pb[c, x, here, :]
            current = retain * jb[c, x, here, :] + pulling * field - spring * polar
            jb[c, x, here, :] = current
            pb[c, x, here, :] = polar + DT * current
            eb[c, x, here, :] = field + step_e * (curl[c] - current)

    def over(update, xs, start, size):
        def body(b, carry):
            y = pl.multiple_of(start + b * ROWS, ROWS)
            for x in xs:
                update(x, y)
            return carry

        lax.fori_loop(0, size // ROWS, body, 0)

    def record(n, buf, base, first):
        for c in range(2):
            total = jnp.zeros((pick.shape[0], width), F32)
            for x in range(layers):
                value = buf[c, x, pl.ds(base, width), :]
                high = value.astype(BF16)
                low = (value - high.astype(F32)).astype(BF16)
                total = total + lax.dot_general(
                    pick[:, pl.ds(x * 2 * deep, 2 * deep)],
                    jnp.concatenate([high, low], axis=1),
                    (((1,), (1,)), ((), ())),
                    preferred_element_type=F32,
                )
            planes[n, first + c] = total

    def step(n, carry):
        over(update_h, range(top), 0, width)
        for c in range(CHUNKS):

            @pl.when(has_upper)
            def _(c=c):
                send_e(c, eb).wait_recv()

                @pl.when(n > 0)
                def _():
                    send_h(c).wait_send()

            over(update_h, [top], c * chunk, chunk)

            @pl.when(has_upper)
            def _(c=c):
                send_h(c).start()

        record(n, hb, PAD, 2)
        over(update_e, range(1, layers), 0, width)
        for c in range(CHUNKS):

            @pl.when(has_lower)
            def _(c=c):
                send_h(c).wait_recv()
                send_e(c, eb).wait_send()

            over(update_e, [0], c * chunk, chunk)

            @pl.when(has_lower & (n < STEPS - 1))
            def _(c=c):
                send_e(c, eb).start()

        record(n, eb, 0, 0)
        return carry

    lax.fori_loop(0, STEPS, step, 0)

    @pl.when(has_upper)
    def _():
        for c in range(CHUNKS):
            send_h(c).wait_send()

    stores = [
        pltpu.make_async_copy(eb.at[:, :, pl.ds(0, width)], el_out, out_sem.at[0]),
        pltpu.make_async_copy(hb.at[:, :, pl.ds(PAD, width)], ma_out, out_sem.at[1]),
    ]
    for store in stores:
        store.start()

    lane = lax.broadcasted_iota(jnp.int32, (nm, deep), 1)
    total = jnp.zeros((nm, deep), F32)
    for c in range(4):
        weights = [mode_ref[3 - c, m] for m in range(nm)]
        for n in range(STEPS):
            sums = []
            for m in range(nm):
                product = planes[n, c, pl.ds(8 * m, layers), :] * weights[m]
                sums.append(jnp.sum(product, axis=0, keepdims=True))
            value = jnp.sum(jnp.concatenate(sums, axis=0), axis=1, keepdims=True)
            value = value if c in (0, 3) else -value
            total = jnp.where(lane == n * 4 + c, value, total)
    part[pl.ds(0, nm), :] = total
    part[pl.ds(nm, 8 - nm), :] = jnp.zeros((8 - nm, deep), F32)

    def share(k, slot):
        return pltpu.make_async_remote_copy(
            src_ref=part,
            dst_ref=gathered.at[slot],
            send_sem=sp_sem.at[k],
            recv_sem=rp_sem.at[k],
            device_id={"gx": lax.rem(me + k, count)},
            device_id_type=MESH,
        )

    for k in range(1, count):
        share(k, me).start()
    gathered[me] = part[...]

    nf = rot_ref.shape[1] // (2 * STEPS)
    for c in range(4):
        half = c // 2
        for m in range(nm):
            plane = [planes[n, c, pl.ds(8 * m, layers), :] for n in range(STEPS)]
            for r in range(2):
                for f in range(nf):
                    value = rot_ref[r, (half * STEPS) * nf + f] * plane[0]
                    for n in range(1, STEPS):
                        value = value + rot_ref[r, (half * STEPS + n) * nf + f] * plane[n]
                    mon_ref[r, c, f, m] = value

    for k in range(1, count):
        share(k, lax.rem(me - k + count, count)).wait()
    full = gathered[0]
    for k in range(1, count):
        full = full + gathered[k]
    for r in range(2):
        out = lax.dot_general(
            full,
            rotv_ref[r],
            (((1,), (1,)), ((), ())),
            preferred_element_type=F32,
            precision=lax.Precision.HIGHEST,
        )
        inter_ref[r] = scale * out[:nm, :]
    for store in stores:
        store.wait()


def on_device(
    electric,
    magnetic,
    material,
    permittivity,
    pole_frequency,
    pole_damping,
    pole_strength,
    frequencies,
    plane_depth,
    mode_fields,
):
    count = lax.axis_size("gx")
    layers, width, deep = material.shape
    nm, nf = plane_depth.shape[0], frequencies.shape[0]
    scale = 1.0 / math.sqrt(4.0 * layers * count * width)
    step = jnp.arange(STEPS, dtype=F32)
    times = jnp.stack([(step + 1.0) * DT, (step + 0.5) * DT])
    phase = times[:, :, None] * frequencies[None, None, :]
    rot = jnp.stack([jnp.cos(phase), -jnp.sin(phase)])
    table = rot.reshape(2, 2 * STEPS * nf)
    lanes = jnp.repeat(rot, 2, axis=1).transpose(0, 3, 2, 1).reshape(2, nf, STEPS * 4)
    lanes = jnp.pad(lanes, ((0, 0), (0, 0), (0, deep - STEPS * 4)))

    smem = pl.BlockSpec(memory_space=pltpu.SMEM)
    vmem = pl.BlockSpec(memory_space=pltpu.VMEM)
    hbm = pl.BlockSpec(memory_space=pl.ANY)
    field = (3, layers, width, deep)
    dma = pltpu.SemaphoreType.DMA
    return pl.pallas_call(
        functools.partial(main_kernel, count, scale),
        out_shape=(
            jax.ShapeDtypeStruct(field, F32),
            jax.ShapeDtypeStruct(field, F32),
            jax.ShapeDtypeStruct((2, 4, nf, nm, layers, width), F32),
            jax.ShapeDtypeStruct((2, nm, nf), F32),
        ),
        in_specs=[smem] * 6 + [vmem] * 2 + [hbm] * 3,
        out_specs=(hbm, hbm, vmem, vmem),
        scratch_shapes=[
            pltpu.VMEM((3, layers, width + PAD, deep), F32),
            pltpu.VMEM((3, layers, width + PAD, deep), F32),
            pltpu.VMEM((2, width, deep), F32),
            pltpu.VMEM((2, width, deep), F32),
            pltpu.VMEM(field, F32),
            pltpu.VMEM(field, F32),
            pltpu.VMEM((4, layers, width, deep), F32),
            pltpu.VMEM((layers, width, deep), jnp.int32),
            pltpu.VMEM((STEPS, 4, 8 * nm, width), F32),
            pltpu.VMEM((8 * nm, layers * 2 * deep), BF16),
            pltpu.VMEM((8, deep), F32),
            pltpu.VMEM((count, 8, deep), F32),
            dma((3,)),
            dma((2,)),
            dma((CHUNKS,)),
            dma((CHUNKS,)),
            dma((CHUNKS,)),
            dma((CHUNKS,)),
            dma((count,)),
            dma((count,)),
        ],
        compiler_params=pltpu.CompilerParams(collective_id=0, has_side_effects=True),
    )(
        permittivity,
        pole_frequency,
        pole_damping,
        pole_strength,
        plane_depth,
        table,
        lanes,
        mode_fields,
        electric,
        magnetic,
        material,
    )


def solution(mesh):
    in_specs = (
        P(None, "gx", None, None),
        P(None, "gx", None, None),
        P(("member", "gx"), None, None),
        P(),
        P(),
        P(),
        P(),
        P(),
        P(),
        P(None, None, "gx", None),
    )
    out_specs = (
        P(None, ("member", "gx"), None, None),
        P(None, ("member", "gx"), None, None),
        P(None, None, None, None, ("member", "gx"), None),
        P("member", None, None),
    )
    return jax.shard_map(
        on_device, mesh=mesh, in_specs=in_specs, out_specs=out_specs, check_vma=False
    )
```

```python
import functools
import math

import jax
import jax.numpy as jnp
from jax import lax
from jax.experimental import pallas as pl
from jax.experimental.pallas import tpu as pltpu
from jax.sharding import PartitionSpec as P

STEPS = 6
DT = 0.5
CHUNKS = 8
ROWS = 32
PAD = 8
MESH = pl.DeviceIdType.MESH
VMEM_BYTES = 67043328
F32 = jnp.float32
BF16 = jnp.bfloat16


def ahead(value):
    width = value.shape[-1]
    lane = lax.broadcasted_iota(jnp.int32, value.shape, 1)
    return jnp.where(lane == width - 1, 0.0, pltpu.roll(value, width - 1, 1))


def behind(value):
    lane = lax.broadcasted_iota(jnp.int32, value.shape, 1)
    return jnp.where(lane == 0, 0.0, pltpu.roll(value, 1, 1))


def main_kernel(
    count,
    scale,
    perm_ref,
    freq_ref,
    damp_ref,
    strength_ref,
    omega_ref,
    depth_ref,
    mode_ref,
    el_ref,
    ma_ref,
    mat_ref,
    eb,
    hb,
    mon_ref,
    inter_ref,
    ge,
    gh,
    jb,
    pb,
    coef,
    matb,
    planes,
    pick,
    part,
    gathered,
    rot,
    rot_s,
    in_sem,
    rot_sem,
    se_sem,
    re_sem,
    sh_sem,
    rh_sem,
    sp_sem,
    rp_sem,
):
    me = lax.axis_index("gx")
    layers, width, deep = mat_ref.shape
    nm, nf = depth_ref.shape[0], omega_ref.shape[0]
    chunk = width // CHUNKS
    has_upper = me < count - 1
    has_lower = me > 0
    top = layers - 1

    barrier = pltpu.get_barrier_semaphore()
    for k in range(1, count):
        pl.semaphore_signal(
            barrier, inc=1, device_id={"gx": lax.rem(me + k, count)}, device_id_type=MESH
        )

    loads = [
        pltpu.make_async_copy(el_ref, eb.at[:, :, pl.ds(0, width)], in_sem.at[0]),
        pltpu.make_async_copy(ma_ref, hb.at[:, :, pl.ds(PAD, width)], in_sem.at[1]),
        pltpu.make_async_copy(mat_ref, matb, in_sem.at[2]),
    ]
    for load in loads:
        load.start()

    def send_e(c, source):
        rows = pl.ds(c * chunk, chunk)
        return pltpu.make_async_remote_copy(
            src_ref=source.at[pl.ds(1, 2), 0, rows],
            dst_ref=ge.at[:, rows],
            send_sem=se_sem.at[c],
            recv_sem=re_sem.at[c],
            device_id={"gx": me - 1},
            device_id_type=MESH,
        )

    def send_h(c):
        return pltpu.make_async_remote_copy(
            src_ref=hb.at[pl.ds(1, 2), top, pl.ds(PAD + c * chunk, chunk)],
            dst_ref=gh.at[:, pl.ds(c * chunk, chunk)],
            send_sem=sh_sem.at[c],
            recv_sem=rh_sem.at[c],
            device_id={"gx": me + 1},
            device_id_type=MESH,
        )

    shape = pick.shape
    row = lax.broadcasted_iota(jnp.int32, shape, 0)
    col = lax.broadcasted_iota(jnp.int32, shape, 1)
    wanted = jnp.zeros(shape, jnp.int32)
    for m in range(nm):
        wanted = jnp.where(row // 8 == m, depth_ref[m], wanted)
    hit = (row % 8 == col // (2 * deep)) & (col % deep == wanted)
    pick[...] = jnp.where(hit, 1.0, 0.0).astype(BF16)

    lane = lax.broadcasted_iota(jnp.int32, (nf, deep), 1)
    line = lax.broadcasted_iota(jnp.int32, (nf, deep), 0)
    omega = jnp.zeros((nf, deep), F32)
    for f in range(nf):
        omega = jnp.where(line == f, omega_ref[f], omega)
    late = jnp.where(lane % 4 < 2, 1.0, 0.5)
    phase = ((lane // 4).astype(F32) + late) * DT * omega
    rot[0] = jnp.where(lane < 4 * STEPS, jnp.cos(phase), 0.0)
    rot[1] = jnp.where(lane < 4 * STEPS, -jnp.sin(phase), 0.0)

    zero_rows = jnp.zeros((PAD, deep), F32)
    for c in range(3):
        for x in range(layers):
            eb[c, x, pl.ds(width, PAD), :] = zero_rows
            hb[c, x, pl.ds(0, PAD), :] = zero_rows
    part[...] = jnp.zeros_like(part)

    pl.semaphore_wait(barrier, count - 1)

    @pl.when(has_lower)
    def _():
        for c in range(CHUNKS):
            send_e(c, el_ref).start()

    kinds = perm_ref.shape[0]
    offset = kinds - freq_ref.shape[0]
    ones = jnp.ones((8, deep), F32)
    tables = []
    for kind in range(kinds):
        if kind < offset:
            g, w2, drive = 0.0 * ones, 0.0 * ones, 0.0 * ones
        else:
            p = kind - offset
            g = damp_ref[p] * ones
            w2 = (freq_ref[p] * ones) * freq_ref[p]
            drive = strength_ref[p] * w2
        divisor = 1.0 + 0.5 * DT * g
        tables.append(
            (
                (1.0 - 0.5 * DT * g) / divisor,
                DT * drive / divisor,
                DT * w2 / divisor,
                DT / (perm_ref[kind] * ones),
            )
        )

    loads[2].wait()
    for x in range(layers):

        def fill(b, carry, x=x):
            rows = pl.ds(pl.multiple_of(b * 8, 8), 8)
            q = matb[x, rows, :]
            for i in range(4):
                value = tables[0][i]
                for kind in range(1, kinds):
                    value = jnp.where(q == kind, tables[kind][i], value)
                coef[i, x, rows, :] = value
            zero = jnp.zeros_like(ones)
            for c in range(3):
                jb[c, x, rows, :] = zero
                pb[c, x, rows, :] = zero
            return carry

        lax.fori_loop(0, width // 8, fill, 0, unroll=2)

    loads[0].wait()
    loads[1].wait()

    def update_h(x, y, size):
        here, next_y = pl.ds(y, size), pl.ds(y + 1, size)
        spot = pl.ds(y + PAD, size)
        ex, ey, ez = eb[0, x, here, :], eb[1, x, here, :], eb[2, x, here, :]
        ex_y, ez_y = eb[0, x, next_y, :], eb[2, x, next_y, :]
        hb[0, x, spot, :] -= DT * ((ez_y - ez) - (ahead(ey) - ey))
        if x < top:
            ey_x, ez_x = eb[1, x + 1, here, :], eb[2, x + 1, here, :]
            hb[1, x, spot, :] -= DT * ((ahead(ex) - ex) - (ez_x - ez))
            hb[2, x, spot, :] -= DT * ((ey_x - ey) - (ex_y - ex))
        else:
            hb[1, x, spot, :] -= DT * ((ahead(ex) - ex) + ez)
            hb[2, x, spot, :] += DT * (ey + (ex_y - ex))

    def finish_h(y, size):
        here, spot = pl.ds(y, size), pl.ds(y + PAD, size)
        hb[1, top, spot, :] += DT * ge[1, here, :]
        hb[2, top, spot, :] -= DT * ge[0, here, :]

    def update_e(x, y, size):
        here = pl.ds(y, size)
        spot, last_y = pl.ds(y + PAD, size), pl.ds(y + PAD - 1, size)
        hx, hy, hz = hb[0, x, spot, :], hb[1, x, spot, :], hb[2, x, spot, :]
        hx_y, hz_y = hb[0, x, last_y, :], hb[2, x, last_y, :]
        if x > 0:
            dz = hz - hb[2, x - 1, spot, :]
            dy = hy - hb[1, x - 1, spot, :]
        else:
            dz, dy = hz, hy
        curl = (
            (hz - hz_y) - (hy - behind(hy)),
            (hx - behind(hx)) - dz,
            dy - (hx - hx_y),
        )
        retain, pulling = coef[0, x, here, :], coef[1, x, here, :]
        spring, step_e = coef[2, x, here, :], coef[3, x, here, :]
        for c in range(3):
            field, polar = eb[c, x, here, :], pb[c, x, here, :]
            current = retain * jb[c, x, here, :] + pulling * field - spring * polar
            jb[c, x, here, :] = current
            pb[c, x, here, :] = polar + DT * current
            eb[c, x, here, :] = field + step_e * (curl[c] - current)

    def finish_e(y, size):
        here = pl.ds(y, size)
        step_e = coef[3, 0, here, :]
        eb[1, 0, here, :] += step_e * gh[1, here, :]
        eb[2, 0, here, :] -= step_e * gh[0, here, :]

    def edge(update, x):
        def body(b, carry):
            update(x, pl.multiple_of(b * ROWS, ROWS), ROWS)
            return carry

        lax.fori_loop(0, width // ROWS, body, 0)

    def inner(update, xs, c):
        for x in xs:
            for y in range(c * chunk, (c + 1) * chunk, min(ROWS, chunk)):
                update(x, y, min(ROWS, chunk))

    def record(n, buf, base, source, c):
        total = jnp.zeros((pick.shape[0], width), F32)
        for x in range(layers):
            value = buf[source, x, pl.ds(base, width), :]
            high = value.astype(BF16)
            low = (value - high.astype(F32)).astype(BF16)
            total = total + lax.dot_general(
                pick[:, pl.ds(x * 2 * deep, 2 * deep)],
                jnp.concatenate([high, low], axis=1),
                (((1,), (1,)), ((), ())),
                preferred_element_type=F32,
            )
        planes[n, c] = total
        sums = []
        for m in range(nm):
            product = total[8 * m : 8 * m + layers, :] * mode_ref[3 - c, m]
            sums.append(jnp.sum(product, axis=0, keepdims=True))
        value = jnp.sum(jnp.concatenate(sums, axis=0), axis=1, keepdims=True)
        value = value if c in (0, 3) else -value
        here = lax.broadcasted_iota(jnp.int32, (nm, deep), 1) == n * 4 + c
        part[pl.ds(0, nm), :] = jnp.where(here, value, part[pl.ds(0, nm), :])

    spots = (CHUNKS // 3, (2 * CHUNKS) // 3)

    def step(n, carry):
        @pl.when(has_upper & (n > 0))
        def _():
            for c in range(CHUNKS):
                send_h(c).wait_send()

        edge(update_h, top)
        for c in range(CHUNKS):

            @pl.when(has_upper)
            def _(c=c):
                send_e(c, eb).wait_recv()
                finish_h(c * chunk, chunk)
                send_h(c).start()

            inner(update_h, range(top), c)
            if c in spots:

                @pl.when(n > 0)
                def _(c=c):
                    record(n - 1, eb, 0, spots.index(c), spots.index(c))

        @pl.when(has_lower)
        def _():
            for c in range(CHUNKS):
                send_e(c, eb).wait_send()

        edge(update_e, 0)
        for c in range(CHUNKS):

            @pl.when(has_lower)
            def _(c=c):
                send_h(c).wait_recv()
                finish_e(c * chunk, chunk)

                @pl.when(n < STEPS - 1)
                def _():
                    send_e(c, eb).start()

            inner(update_e, range(1, layers), c)
            if c in spots:
                record(n, hb, PAD, spots.index(c), 2 + spots.index(c))
        return carry

    lax.fori_loop(0, STEPS, step, 0)

    for c in range(2):
        record(STEPS - 1, eb, 0, c, c)

    def share(k, slot):
        return pltpu.make_async_remote_copy(
            src_ref=part,
            dst_ref=gathered.at[slot],
            send_sem=sp_sem.at[k],
            recv_sem=rp_sem.at[k],
            device_id={"gx": lax.rem(me + k, count)},
            device_id_type=MESH,
        )

    for k in range(1, count):
        share(k, me).start()
    gathered[me] = part[...]

    to_scalars = pltpu.make_async_copy(rot, rot_s, rot_sem)
    to_scalars.start()

    @pl.when(has_upper)
    def _():
        for c in range(CHUNKS):
            send_h(c).wait_send()

    to_scalars.wait()
    for c in range(4):

        def fold(m, carry, c=c):
            rows = pl.ds(pl.multiple_of(8 * m, 8), layers)
            plane = [planes[n, c, rows, :] for n in range(STEPS)]
            for r in range(2):
                for f in range(nf):
                    value = rot_s[r, f, c] * plane[0]
                    for n in range(1, STEPS):
                        value = value + rot_s[r, f, n * 4 + c] * plane[n]
                    mon_ref[r, c, f, m] = value
            return carry

        lax.fori_loop(0, nm, fold, 0)

    for k in range(1, count):
        share(k, lax.rem(me - k + count, count)).wait()
    full = gathered[0]
    for k in range(1, count):
        full = full + gathered[k]
    for r in range(2):
        out = lax.dot_general(
            full,
            rot[r],
            (((1,), (1,)), ((), ())),
            preferred_element_type=F32,
            precision=lax.Precision.HIGHEST,
        )
        inter_ref[r] = scale * out[:nm, :]


def place_kernel(eb, hb, mon, inter, el_out, ma_out, mon_out, inter_out, sems):
    width = el_out.shape[2]
    copies = [
        pltpu.make_async_copy(eb.at[:, :, pl.ds(0, width)], el_out, sems.at[0]),
        pltpu.make_async_copy(hb.at[:, :, pl.ds(PAD, width)], ma_out, sems.at[1]),
        pltpu.make_async_copy(mon, mon_out, sems.at[2]),
        pltpu.make_async_copy(inter, inter_out, sems.at[3]),
    ]
    for copy in copies:
        copy.start()
    for copy in copies:
        copy.wait()


def on_device(
    electric,
    magnetic,
    material,
    permittivity,
    pole_frequency,
    pole_damping,
    pole_strength,
    frequencies,
    plane_depth,
    mode_fields,
):
    count = lax.axis_size("gx")
    layers, width, deep = material.shape
    nm, nf = plane_depth.shape[0], frequencies.shape[0]
    scale = 1.0 / math.sqrt(4.0 * layers * count * width)

    smem = pl.BlockSpec(memory_space=pltpu.SMEM)
    vmem = pl.BlockSpec(memory_space=pltpu.VMEM)
    hbm = pl.BlockSpec(memory_space=pl.ANY)
    field = (3, layers, width, deep)
    padded = (3, layers, width + PAD, deep)
    final = (field, field, (2, 4, nf, nm, layers, width), (2, nm, nf))
    kept = 4 * (2 * math.prod(padded) + math.prod(final[2])) + 2**16
    dma = pltpu.SemaphoreType.DMA
    held = pl.pallas_call(
        functools.partial(main_kernel, count, scale),
        out_shape=tuple(pltpu.VMEM(shape, F32) for shape in (padded, padded) + final[2:]),
        in_specs=[smem] * 6 + [vmem] + [hbm] * 3,
        out_specs=(vmem,) * 4,
        scratch_shapes=[
            pltpu.VMEM((2, width, deep), F32),
            pltpu.VMEM((2, width, deep), F32),
            pltpu.VMEM(field, F32),
            pltpu.VMEM(field, F32),
            pltpu.VMEM((4, layers, width, deep), F32),
            pltpu.VMEM((layers, width, deep), jnp.int32),
            pltpu.VMEM((STEPS, 4, 8 * nm, width), F32),
            pltpu.VMEM((8 * nm, layers * 2 * deep), BF16),
            pltpu.VMEM((8, deep), F32),
            pltpu.VMEM((count, 8, deep), F32),
            pltpu.VMEM((2, nf, deep), F32),
            pltpu.SMEM((2, nf, deep), F32),
            dma((3,)),
            dma,
            dma((CHUNKS,)),
            dma((CHUNKS,)),
            dma((CHUNKS,)),
            dma((CHUNKS,)),
            dma((count,)),
            dma((count,)),
        ],
        compiler_params=pltpu.CompilerParams(
            collective_id=0, has_side_effects=True, vmem_limit_bytes=VMEM_BYTES - kept
        ),
    )(
        permittivity,
        pole_frequency,
        pole_damping,
        pole_strength,
        frequencies,
        plane_depth,
        mode_fields,
        *(pltpu.with_memory_space_constraint(a, pltpu.HBM) for a in (electric, magnetic, material)),
    )
    return pl.pallas_call(
        place_kernel,
        out_shape=tuple(jax.ShapeDtypeStruct(shape, F32) for shape in final),
        in_specs=[vmem] * 4,
        out_specs=(hbm,) * 4,
        scratch_shapes=[dma((4,))],
        compiler_params=pltpu.CompilerParams(vmem_limit_bytes=16 * 2**20),
    )(*held)


def solution(mesh):
    in_specs = (
        P(None, "gx", None, None),
        P(None, "gx", None, None),
        P(("member", "gx"), None, None),
        P(),
        P(),
        P(),
        P(),
        P(),
        P(),
        P(None, None, "gx", None),
    )
    out_specs = (
        P(None, ("member", "gx"), None, None),
        P(None, ("member", "gx"), None, None),
        P(None, None, None, None, ("member", "gx"), None),
        P("member", None, None),
    )
    return jax.shard_map(
        on_device, mesh=mesh, in_specs=in_specs, out_specs=out_specs, check_vma=False
    )
```
